32 devices in a mesh: tile: 8 (over y, x, core), scen: 4 (over z).
Axes of the slice: x: 2, y: 2, z: 4, core: 2. Of those that a mesh axis runs over, the one named last changes fastest.
Arguments:
- terrain: bfloat16 [4, 48, 64, 768], P('scen', 'tile'), may hold values from -6 to 6
- kernel: float32 [7, 7, 768], replicated, may hold values from -0.875 to 0.875
- w_in: bfloat16 [768, 1536], P(None, 'scen'), may hold values from -0.21875 to 0.21875
- w_out: bfloat16 [1536, 768], P('scen'), may hold values from -0.15625 to 0.15625
- cotangent: bfloat16 [4, 48, 64, 768], P('scen', 'tile'), may hold values from -6 to 6
Outputs:
- output: bfloat16 [4, 48, 64, 768], P('scen', 'tile')
- d_terrain: bfloat16 [4, 48, 64, 768], P('scen', 'tile')
- grad_in: float32 [768, 1536], P(None, 'scen')
The draws below stay inside these ranges and needn't reach their ends.
All inputs are finite; a program needn't handle non-finite values.
Results may differ from the reference program's by a relative error of at most 0.0085.
Values may be sent and summed in bfloat16 or wider, within the bound.
No kernel may reach another device: no remote copies, remote signals or barrier semaphores. Data moves between devices by JAX's collectives and lax.ppermute only.
A program may use at most 64 MiB of HBM per device.

```python
import math
import jax
import jax.numpy as jnp
from jax import lax

C = 768
HID = 1536
RD = 6
COLS = 64
NR = 48
SCEN = 4
PIXELS = 12288
N_TILE = 8
N_SCEN = 4


def block_scale(own_key, dims, pieces, low, top_value):
    level = 1.0
    for dim, shards_of in pieces:
        steps = jax.random.uniform(jax.random.fold_in(jax.random.fold_in(own_key, 6), dim), (shards_of,), jnp.float32, low / len(pieces), top_value / len(pieces))
        level = level * jnp.repeat(jnp.exp(steps), dims[dim] // shards_of).reshape((-1,) + (1,) * (len(dims) - 1 - dim))
    return level


def noise(own_key, extent, scale, bound, pieces=(), held_as=jnp.bfloat16):
    values = scale * jax.random.normal(own_key, extent, jnp.float32)
    if pieces:
        values = values * block_scale(own_key, extent, pieces, -0.22, 0.18)
    return jnp.clip(values, -bound, bound).astype(held_as)


def setup_inputs(seed: int = 0) -> dict:
    arg_keys = jax.random.split(jax.random.key(seed), 6)
    return {
        "terrain": noise(arg_keys[0], (SCEN, NR, COLS, C), 1.0, 6.0, ((0, 4), (1, 8))),
        "kernel": noise(arg_keys[1], (7, 7, C), 49 ** -0.5, 0.875, (), jnp.float32),
        "w_in": noise(arg_keys[2], (C, HID), C ** -0.5, 0.21875, ((1, 4),)),
        "w_out": noise(arg_keys[3], (HID, C), HID ** -0.5, 0.15625, ((0, 4),)),
        "cotangent": noise(arg_keys[4], (SCEN, NR, COLS, C), 1.0, 6.0, ((0, 4), (1, 8))),
    }


def depthwise(padded, kernel, height, breadth):
    total = jnp.zeros(padded.shape[:-3] + (height, breadth, padded.shape[-1]), jnp.float32)
    for shift_r in range(7):
        for shift_c in range(7):
            total = total + kernel[shift_r, shift_c] * padded[..., shift_r:shift_r + height, shift_c:shift_c + breadth, :]
    return total

def normal_cdf(values):
    return 0.5 * (1.0 + jax.scipy.special.erf(values * 0.7071067811865476))

def gelu_slope(values):
    return normal_cdf(values) + values * jnp.exp(-0.5 * values * values) * 0.3989422804014327

def reference(terrain, kernel, w_in, w_out, cotangent):
    contract_last = (((1,), (1,)), ((), ()))
    contract_first = (((0,), (0,)), ((), ()))
    pad_both = ((3, 3), (3, 3), (0, 0))
    outputs = []
    d_inputs = []
    grad_sum = jnp.zeros((C, HID), jnp.float32)
    for scene in range(N_SCEN):
        source = terrain[scene].astype(jnp.float32)
        conv_out = depthwise(jnp.pad(source, pad_both), kernel, NR, COLS)
        mean_u = lax.optimization_barrier(jnp.mean(conv_out, -1, keepdims=True))
        centred = conv_out - mean_u
        inv_std = lax.rsqrt(lax.optimization_barrier(jnp.mean(centred * centred, -1, keepdims=True)) + 1e-06)
        normed = centred * inv_std
        normed_bf = normed.astype(jnp.bfloat16).reshape(-1, C)
        pre = jnp.dot(normed_bf, w_in, preferred_element_type=jnp.float32)
        activ = (pre * normal_cdf(pre)).astype(jnp.bfloat16)
        mixed = jnp.dot(activ, w_out, preferred_element_type=jnp.float32)
        outputs.append((source.reshape(-1, C) + mixed).astype(jnp.bfloat16).reshape(NR, COLS, C))
        upstream = cotangent[scene].reshape(-1, C)
        d_hidden = lax.dot_general(upstream, w_out, contract_last, preferred_element_type=jnp.float32)
        d_pre = (d_hidden * gelu_slope(pre)).astype(jnp.bfloat16)
        d_normed = lax.dot_general(d_pre, w_in, contract_last, preferred_element_type=jnp.float32).reshape(NR, COLS, C)
        mean_d = lax.optimization_barrier(jnp.mean(d_normed, -1, keepdims=True))
        mean_dn = lax.optimization_barrier(jnp.mean(d_normed * normed, -1, keepdims=True))
        d_conv = (inv_std * (d_normed - mean_d - normed * mean_dn)).astype(jnp.bfloat16)
        back = depthwise(jnp.pad(d_conv.astype(jnp.float32), pad_both), kernel[::-1, ::-1], NR, COLS)
        d_inputs.append((cotangent[scene].astype(jnp.float32) + back).astype(jnp.bfloat16))
        normed_groups = normed_bf.reshape(N_TILE, RD * COLS, C)
        pre_groups = d_pre.reshape(N_TILE, RD * COLS, HID)

        def accumulate(carry, pair):
            partial_value = lax.dot_general(pair[0], pair[1], contract_first, preferred_element_type=jnp.float32)
            rounded = lax.optimization_barrier(partial_value.astype(jnp.bfloat16)).astype(jnp.float32)
            return (carry + rounded, None)
        grad_sum, _ = lax.scan(accumulate, grad_sum, (normed_groups, pre_groups))
    grad_in = grad_sum * (1.0 / math.sqrt(PIXELS))
    return (jnp.stack(outputs), jnp.stack(d_inputs), grad_in)
```

```python
import functools
import math

import jax
import jax.numpy as jnp
from jax import lax
from jax.experimental import pallas as pl
from jax.experimental.pallas import tpu as pltpu
from jax.sharding import PartitionSpec as P

LANES = 128
SUB = 8
PACK = 16
VMEM = pl.BlockSpec(memory_space=pltpu.VMEM)
ANY = pl.BlockSpec(memory_space=pl.ANY)
F32 = jnp.float32
BF16 = jnp.bfloat16


def group_size(tiles, channels, shard):
    g = 1
    while tiles % (2 * g) == 0 and channels % (2 * g * PACK) == 0 and shard % (2 * g * PACK) == 0:
        g *= 2
    return g


class Exchange:
    def __init__(self, tiles, scens, g):
        self.tiles, self.scens, self.g = tiles, scens, g
        self.bits = [1 << i for i in range(1, g.bit_length() - 1)]
        self.stages = len(self.bits)

    def stage_mask(self, j, parity):
        return self.bits[j] if parity == 0 else self.bits[self.stages - 1 - j]

    def stage(self, x, j):
        perm = [(t, t ^ self.stage_mask(j, t % 2)) for t in range(self.tiles)]
        return lax.ppermute(x, "tile", perm)

    def core(self, x):
        return lax.ppermute(x, "tile", [(t, t ^ 1) for t in range(self.tiles)])

    def plane(self, z, r):
        if self.scens & (self.scens - 1) == 0:
            return z ^ r
        return (z + r) % self.scens

    def fetch(self, x, r):
        return lax.ppermute(x, "scen", [(self.plane(z, r), z) for z in range(self.scens)])

    def deliver(self, x, r):
        return lax.ppermute(x, "scen", [(z, self.plane(z, r)) for z in range(self.scens)])

    def gather(self, x):
        items = [(x, (0, 0))]
        for j in range(self.stages):
            m0, m1 = self.stage_mask(j, 0), self.stage_mask(j, 1)
            items += [(self.stage(a, j), (o[0] ^ m0, o[1] ^ m1)) for a, o in items]
        if self.g > 1:
            items += [(self.core(a), (1 ^ o[1], 1 ^ o[0])) for a, o in items]
        return [a for a, _ in items], [o for _, o in items]

    def slots(self):
        count = 1 << self.stages
        offs = []
        for idx in range(count):
            o = [0, 0]
            for j in range(self.stages):
                if idx >> (self.stages - 1 - j) & 1:
                    o[0] ^= self.stage_mask(j, 0)
                    o[1] ^= self.stage_mask(j, 1)
            offs.append(tuple(o))
        return offs, [(1 ^ o[1], 1 ^ o[0]) for o in offs]


def member(g):
    t = lax.axis_index("tile")
    return lax.rem(t, g), lax.rem(t, 2)


def place(me, parity, off):
    return me ^ jnp.where(parity == 0, off[0], off[1])


def normal_cdf(values):
    return 0.5 * (1.0 + lax.erf(values * 0.7071067811865476))


def contract(a, b, da, db):
    return lax.dot_general(a, b, (((da,), (db,)), ((), ())), preferred_element_type=F32)


def fill_padded(xs, before, mid, after, rows, rad, cols, lanes):
    xs[0:rad, SUB : SUB + cols, :] = before[:, :, lanes].astype(F32)
    xs[rad : rad + rows, SUB : SUB + cols, :] = mid[:, :, lanes].astype(F32)
    xs[rad + rows : rows + 2 * rad, SUB : SUB + cols, :] = after[:, :, lanes].astype(F32)


def zero_edges(xs, rows, rad, cols):
    edge = jnp.zeros((rows + 2 * rad, SUB, LANES), F32)
    xs[:, 0:SUB, :] = edge
    xs[:, SUB + cols : 2 * SUB + cols, :] = edge


def taps(xs, kb, out, rows, rad, cols, flip):
    width = 2 * rad + 1
    per = cols // SUB
    step = 4 if per % 4 == 0 else 1
    for j0 in range(0, per, step):
        acc = [[None] * step for _ in range(rows)]
        for b in range(width):
            for src in range(rows + 2 * rad):
                xv = [
                    xs[src, pl.ds(SUB + j0 + j + b - rad, SUB, stride=per), :] for j in range(step)
                ]
                for r in range(rows):
                    a = src - r
                    if 0 <= a < width:
                        k = kb[width * width - 1 - (a * width + b)] if flip else kb[a * width + b]
                        for j in range(step):
                            term = k * xv[j]
                            acc[r][j] = term if acc[r][j] is None else acc[r][j] + term
        for r in range(rows):
            for j in range(step):
                out[r, pl.ds(j0 + j, SUB, stride=per), :] = acc[r][j]


def spread_taps(kb, kernel_ref, lanes, width):
    for a in range(width):
        row = kernel_ref[a, :, lanes]
        for b in range(width):
            kb[a * width + b] = jnp.broadcast_to(row[b : b + 1], (SUB, LANES))


def forward_conv_kernel(
    before, mid, after, kernel_ref, normed_bf, normed, inv_out, xs, kb, conv
):
    rows, cols, channels = mid.shape
    rad = before.shape[0]
    blocks = channels // LANES
    zero_edges(xs, rows, rad, cols)

    def block(cb, _):
        lanes = pl.ds(pl.multiple_of(cb * LANES, LANES), LANES)
        fill_padded(xs, before, mid, after, rows, rad, cols, lanes)
        spread_taps(kb, kernel_ref, lanes, 2 * rad + 1)
        taps(xs, kb, conv.at[cb], rows, rad, cols, False)
        return 0

    lax.fori_loop(0, blocks, block, 0)

    def norm(r, _):
        total = conv[0, r]
        for cb in range(1, blocks):
            total = total + conv[cb, r]
        mean_u = jnp.sum(total, -1, keepdims=True) * (1.0 / channels)
        square = jnp.zeros((cols, LANES), F32)
        for cb in range(blocks):
            centred = conv[cb, r] - mean_u
            square = square + centred * centred
        var = jnp.sum(square, -1, keepdims=True) * (1.0 / channels)
        inv_std = lax.rsqrt(var + 1e-06)
        for cb in range(blocks):
            value = (conv[cb, r] - mean_u) * inv_std
            normed[r, :, cb * LANES : (cb + 1) * LANES] = value
            normed_bf[r, :, cb * LANES : (cb + 1) * LANES] = value.astype(BF16)
        inv_out[r] = inv_std
        return 0

    lax.fori_loop(0, rows, norm, 0)


def backward_conv_kernel(before, mid, after, kernel_ref, cot, out, xs, kb, conv):
    rows, cols, channels = mid.shape
    rad = before.shape[0]
    zero_edges(xs, rows, rad, cols)

    def block(cb, _):
        lanes = pl.ds(pl.multiple_of(cb * LANES, LANES), LANES)
        fill_padded(xs, before, mid, after, rows, rad, cols, lanes)
        spread_taps(kb, kernel_ref, lanes, 2 * rad + 1)
        taps(xs, kb, conv, rows, rad, cols, True)
        out[:, :, lanes] = (cot[:, :, lanes].astype(F32) + conv[...]).astype(BF16)
        return 0

    lax.fori_loop(0, channels // LANES, block, 0)


def conv_scratch(rows, rad, cols):
    width = 2 * rad + 1
    return [
        pltpu.VMEM((rows + 2 * rad, cols + 2 * SUB, LANES), F32),
        pltpu.VMEM((width * width, SUB, LANES), F32),
    ]


def forward_conv(before, mid, after, kernel):
    rows, cols, channels = mid.shape
    rad = before.shape[0]
    return pl.pallas_call(
        forward_conv_kernel,
        name="forward_conv",
        out_shape=(
            jax.ShapeDtypeStruct(mid.shape, BF16),
            jax.ShapeDtypeStruct(mid.shape, F32),
            jax.ShapeDtypeStruct((rows, cols, 1), F32),
        ),
        in_specs=[VMEM] * 4,
        out_specs=(VMEM,) * 3,
        scratch_shapes=conv_scratch(rows, rad, cols)
        + [pltpu.VMEM((channels // LANES, rows, cols, LANES), F32)],
        cost_estimate=pl.CostEstimate(
            flops=2 * mid.size * kernel.shape[0] * kernel.shape[1],
            bytes_accessed=8 * mid.size,
            transcendentals=0,
        ),
    )(before, mid, after, kernel)


def backward_conv(before, mid, after, kernel, cot):
    rows, cols, channels = mid.shape
    rad = before.shape[0]
    return pl.pallas_call(
        backward_conv_kernel,
        name="backward_conv",
        out_shape=jax.ShapeDtypeStruct(mid.shape, BF16),
        in_specs=[VMEM] * 5,
        out_specs=VMEM,
        scratch_shapes=conv_scratch(rows, rad, cols) + [pltpu.VMEM((rows, cols, LANES), F32)],
        cost_estimate=pl.CostEstimate(
            flops=2 * mid.size * kernel.shape[0] * kernel.shape[1],
            bytes_accessed=6 * mid.size,
            transcendentals=0,
        ),
    )(before, mid, after, kernel, cot)


def weight_copies(own_in, own_out, pieces, offs, win, wout, sem, g):
    me, parity = member(g)
    parts, rows, shard = win.shape[1:]
    ratio = parts // g
    copies = [[] for _ in range(win.shape[0])]

    def add(r, src, dst):
        copies[r].append(pltpu.make_async_copy(src, dst, sem.at[r]))

    add(0, own_in, win.at[0])
    add(0, own_out, wout.at[0])
    for r in range(1, win.shape[0]):
        for piece, off in zip(pieces, offs):
            pos = place(me, parity, off)
            for q in range(ratio):
                add(r, piece.at[r - 1, 0, :, pl.ds(q * shard, shard)], win.at[r, pos * ratio + q])
            add(r, piece.at[r - 1, 1], wout.at[r, pos])
    return copies


def hidden_kernel(offs, slots, g, *refs):
    n = len(offs)
    normed_ref, cot_ref, own_in, own_out = refs[:4]
    pieces = refs[4 : 4 + n]
    activ, d_pre, keep, send, win, wout, grad, sem, out_sem = refs[4 + n :]
    scens = win.shape[0]
    channels = normed_ref.shape[1]
    shard = win.shape[3]
    me, parity = member(g)
    copies = weight_copies(own_in, own_out, pieces, offs, win, wout, sem, g)
    for group in copies:
        for c in group:
            c.start()
    normed = normed_ref[...]
    normed_t = normed.T
    cot = cot_ref[...]
    outs = []
    for r in range(scens):
        for c in copies[r]:
            c.wait()
        w_in = win[r].reshape(channels, shard)
        w_out = wout[r].reshape(shard, channels)
        pre = contract(normed, w_in, 1, 0)
        d_hidden = contract(cot, w_out, 1, 1)
        cdf = normal_cdf(pre)
        activ[r] = (pre * cdf).astype(BF16)
        slope = cdf + pre * jnp.exp(-0.5 * pre * pre) * 0.3989422804014327
        d_p = (d_hidden * slope).astype(BF16)
        d_pre[r] = d_p
        grad[r] = contract(normed_t, d_p, 1, 0).astype(BF16).reshape(grad.shape[1:])
        for target, offsets in zip((keep, send), slots):
            for idx, off in enumerate(offsets):
                c = pltpu.make_async_copy(
                    grad.at[r, place(me, parity, off)], target.at[idx, r], out_sem
                )
                c.start()
                outs.append(c)
    for c in outs:
        c.wait()


def input_grad_kernel(offs, g, *refs):
    n = len(offs)
    activ, d_pre, terrain, normed, inv_std, own_in, own_out = refs[:7]
    pieces = refs[7 : 7 + n]
    output, d_conv, win, wout, sem = refs[7 + n :]
    scens = win.shape[0]
    channels = normed.shape[1]
    shard = win.shape[3]
    copies = weight_copies(own_in, own_out, pieces, offs, win, wout, sem, g)
    for group in copies:
        for c in group:
            c.start()
    mixed = d_normed = None
    for r in range(scens):
        for c in copies[r]:
            c.wait()
        dn = contract(d_pre[r], win[r].reshape(channels, shard), 1, 1)
        mx = contract(activ[r], wout[r].reshape(shard, channels), 1, 0)
        mixed = mx if mixed is None else mixed + mx
        d_normed = dn if d_normed is None else d_normed + dn
    output[...] = (terrain[...].astype(F32) + mixed).astype(BF16)
    unit = normed[...]
    mean_d = jnp.sum(d_normed, -1, keepdims=True) * (1.0 / channels)
    mean_dn = jnp.sum(d_normed * unit, -1, keepdims=True) * (1.0 / channels)
    d_conv[...] = (inv_std[...] * (d_normed - mean_d - unit * mean_dn)).astype(BF16)


def weight_scratch(scens, g, channels, shard):
    rows = shard // g
    return [
        pltpu.VMEM((scens, channels // rows, rows, shard), BF16),
        pltpu.VMEM((scens, g, rows, channels), BF16),
        pltpu.SemaphoreType.DMA((scens,)),
    ]


def hidden_stage(ex, normed, cot, w_in, w_out, pieces, offs):
    pixels, channels = normed.shape
    shard = w_in.shape[1]
    g, scens = ex.g, ex.scens
    keep, send = ex.slots()
    slots = (keep, send) if g > 1 else (keep,)
    part = jax.ShapeDtypeStruct((len(keep), scens, channels // g, shard), BF16)
    per_unit = jax.ShapeDtypeStruct((scens, pixels, shard), BF16)
    win, wout, sem = weight_scratch(scens, g, channels, shard)
    return pl.pallas_call(
        functools.partial(hidden_kernel, offs, slots, g),
        name="hidden_stage",
        out_shape=(per_unit, per_unit, part, part),
        in_specs=[VMEM, VMEM] + [ANY] * (2 + len(pieces)),
        out_specs=(VMEM, VMEM, ANY, ANY),
        scratch_shapes=[
            win,
            wout,
            pltpu.VMEM((scens, g, channels // g, shard), BF16),
            sem,
            pltpu.SemaphoreType.DMA,
        ],
        cost_estimate=pl.CostEstimate(
            flops=6 * pixels * channels * shard * scens,
            bytes_accessed=8 * channels * shard * scens,
            transcendentals=2 * pixels * shard * scens,
        ),
    )(normed, cot, w_in.reshape(win.shape[1:]), w_out.reshape(wout.shape[1:]), *pieces)


def input_grad_stage(ex, activ, d_pre, terrain, normed, inv_std, w_in, w_out, pieces, offs):
    pixels, channels = normed.shape
    shard = w_in.shape[1]
    scratch = weight_scratch(ex.scens, ex.g, channels, shard)
    own = [w_in.reshape(scratch[0].shape[1:]), w_out.reshape(scratch[1].shape[1:])]
    flat = jax.ShapeDtypeStruct((pixels, channels), BF16)
    return pl.pallas_call(
        functools.partial(input_grad_kernel, offs, ex.g),
        name="input_grad_stage",
        out_shape=(flat, flat),
        in_specs=[VMEM] * 5 + [ANY] * (2 + len(pieces)),
        out_specs=(VMEM, VMEM),
        scratch_shapes=scratch,
        cost_estimate=pl.CostEstimate(
            flops=4 * pixels * channels * shard * ex.scens,
            bytes_accessed=8 * channels * shard * ex.scens,
            transcendentals=0,
        ),
    )(activ, d_pre, terrain, normed, inv_std, *own, *pieces)


def final_kernel(offs, g, scale, *refs):
    out = refs[-1]
    me, parity = member(g)
    for block, off in zip(refs[:-1], offs):
        out[place(me, parity, off)] = block[...].astype(F32) * scale


def final_stage(ex, blocks, offs, scale):
    rows, shard = blocks[0].shape
    return pl.pallas_call(
        functools.partial(final_kernel, offs, ex.g, scale),
        name="final_stage",
        out_shape=jax.ShapeDtypeStruct((ex.g, rows, shard), F32),
        in_specs=[VMEM] * len(blocks),
        out_specs=VMEM,
        cost_estimate=pl.CostEstimate(
            flops=ex.g * rows * shard, bytes_accessed=6 * ex.g * rows * shard, transcendentals=0
        ),
    )(*blocks)


def add(a, b):
    return (a.astype(F32) + b.astype(F32)).astype(BF16)


def halo(x, rad):
    peers = lax.axis_size("tile")
    up = [(i, i + 1) for i in range(peers - 1)]
    down = [(j, i) for i, j in up]
    before = lax.ppermute(x[x.shape[0] - rad :], "tile", up)
    after = lax.ppermute(x[:rad], "tile", down)
    return before, after


def shards(terrain, kernel, w_in, w_out, cotangent):
    scenes, height, breadth, channels = terrain.shape
    pixels = scenes * height * breadth
    shard = w_in.shape[1]
    rad = kernel.shape[0] // 2
    tiles, scens = lax.axis_size("tile"), lax.axis_size("scen")
    g = group_size(tiles, channels, shard)
    ex = Exchange(tiles, scens, g)
    me = lax.rem(lax.axis_index("tile"), g)
    rows = shard // g
    ratio = channels // shard

    own = w_in.reshape(g, ratio, rows, shard)[me]
    own = jnp.concatenate([own[q] for q in range(ratio)], axis=-1)
    own = jnp.stack([own, w_out.reshape(g, rows, channels)[me]])
    far = jnp.stack([ex.fetch(own, r) for r in range(1, scens)])
    pieces, offs = ex.gather(far)

    image = terrain.reshape(height, breadth, channels)
    before, after = halo(image, rad)
    normed_bf, normed, inv_std = forward_conv(before, image, after, kernel)
    normed_bf = normed_bf.reshape(pixels, channels)
    normed = normed.reshape(pixels, channels)
    inv_std = inv_std.reshape(pixels, 1)
    cot = cotangent.reshape(pixels, channels)

    activ, d_pre, keep, send = hidden_stage(ex, normed_bf, cot, w_in, w_out, pieces, offs)

    part = add(keep, ex.core(send)) if g > 1 else keep
    for j in range(ex.stages):
        half = part.shape[0] // 2
        part = add(part[:half], ex.stage(part[half:], j))
    part = part[0]
    total = part[0].astype(F32)
    for r in range(1, scens):
        total = total + ex.deliver(part[r], r).astype(F32)
    if tiles > g:
        groups = [[i + g * k for k in range(tiles // g)] for i in range(g)]
        total = lax.psum(total, "tile", axis_index_groups=groups)
    blocks, block_offs = ex.gather(total.astype(BF16))

    output, d_conv = input_grad_stage(
        ex, activ, d_pre, terrain.reshape(pixels, channels), normed, inv_std, w_in, w_out, pieces, offs
    )
    d_image = d_conv.reshape(height, breadth, channels)
    d_before, d_after = halo(d_image, rad)
    d_terrain = backward_conv(
        d_before, d_image, d_after, kernel, cotangent.reshape(height, breadth, channels)
    )

    scale = 1.0 / math.sqrt(pixels * tiles * scens)
    grad_in = final_stage(ex, blocks, block_offs, scale).reshape(channels, shard)
    return output.reshape(terrain.shape), d_terrain.reshape(terrain.shape), grad_in


def solution(mesh):
    return jax.shard_map(
        shards,
        mesh=mesh,
        in_specs=(
            P("scen", "tile", None, None),
            P(),
            P(None, "scen"),
            P("scen", None),
            P("scen", "tile", None, None),
        ),
        out_specs=(P("scen", "tile", None, None), P("scen", "tile", None, None), P(None, "scen")),
        check_vma=False,
    )
```

```python
import functools
import math

import jax
import jax.numpy as jnp
from jax import lax
from jax.experimental import pallas as pl
from jax.experimental.pallas import tpu as pltpu
from jax.sharding import PartitionSpec as P


KERNEL_VMEM = 24 << 20
LANES = 128
SUB = 8
PACK = 16
VMEM = pl.BlockSpec(memory_space=pltpu.VMEM)
ANY = pl.BlockSpec(memory_space=pl.ANY)
F32 = jnp.float32
BF16 = jnp.bfloat16


def group_size(tiles, channels, shard):
    g = 1
    while tiles % (2 * g) == 0 and channels % (2 * g * PACK) == 0 and shard % (2 * g * PACK) == 0:
        g *= 2
    return g


class Exchange:
    def __init__(self, tiles, scens, g):
        self.tiles, self.scens, self.g = tiles, scens, g
        self.bits = [1 << i for i in range(1, g.bit_length() - 1)]
        self.stages = len(self.bits)

    def offset(self, idx, parity):
        off = 0
        for j in range(self.stages):
            if idx >> j & 1:
                off ^= self.bits[j] if parity == 0 else self.bits[self.stages - 1 - j]
        return off

    def chips(self):
        return 1 << self.stages

    def hop(self, x, idx):
        perm = [(t, t ^ self.offset(idx, t % 2)) for t in range(self.tiles)]
        return lax.ppermute(x, "tile", perm)

    def core(self, x):
        return lax.ppermute(x, "tile", [(t, t ^ 1) for t in range(self.tiles)])

    def plane(self, z, r):
        if self.scens & (self.scens - 1) == 0:
            return z ^ r
        return (z + r) % self.scens

    def fetch(self, x, r):
        return lax.ppermute(x, "scen", [(self.plane(z, r), z) for z in range(self.scens)])

    def deliver(self, x, r):
        return lax.ppermute(x, "scen", [(z, self.plane(z, r)) for z in range(self.scens)])

    def keep_offsets(self):
        return [(self.offset(i, 0), self.offset(i, 1)) for i in range(self.chips())]

    def send_offsets(self):
        return [(1 ^ o[1], 1 ^ o[0]) for o in self.keep_offsets()]

    def gather(self, x, direct):
        items = [x]
        if direct:
            items += [self.hop(x, i) for i in range(1, self.chips())]
        else:
            for j in range(self.stages):
                items += [self.hop(a, 1 << j) for a in items]
        offs = self.keep_offsets()
        if self.g > 1:
            items += [self.core(a) for a in items]
            offs = offs + self.send_offsets()
        return items, offs


def member(g):
    t = lax.axis_index("tile")
    return lax.rem(t, g), lax.rem(t, 2)


def place(me, parity, off):
    return me ^ jnp.where(parity == 0, off[0], off[1])


def normal_cdf(values):
    return 0.5 * (1.0 + lax.erf(values * 0.7071067811865476))


def contract(a, b, da, db):
    return lax.dot_general(a, b, (((da,), (db,)), ((), ())), preferred_element_type=F32)


def fill_padded(xs, inner, mid, outer, rows, rad, cols, lanes):
    odd = lax.rem(lax.axis_index("tile"), 2)
    columns = slice(SUB, SUB + cols)
    xs[pl.ds((1 - odd) * (rad + rows), rad), columns, :] = inner[:, :, lanes].astype(F32)
    xs[pl.ds(odd * (rad + rows), rad), columns, :] = outer[:, :, lanes].astype(F32)
    xs[rad : rad + rows, columns, :] = mid[:, :, lanes].astype(F32)


def zero_edges(xs, rows, rad, cols):
    edge = jnp.zeros((rows + 2 * rad, SUB, LANES), F32)
    xs[:, 0:SUB, :] = edge
    xs[:, SUB + cols : 2 * SUB + cols, :] = edge


def taps(xs, kb, out, rows, rad, cols, flip):
    width = 2 * rad + 1
    per = cols // SUB
    step = 4 if per % 4 == 0 else 1
    for j0 in range(0, per, step):
        acc = [[None] * step for _ in range(rows)]
        for b in range(width):
            for src in range(rows + 2 * rad):
                xv = [
                    xs[src, pl.ds(SUB + j0 + j + b - rad, SUB, stride=per), :] for j in range(step)
                ]
                for r in range(rows):
                    a = src - r
                    if 0 <= a < width:
                        k = kb[width * width - 1 - (a * width + b)] if flip else kb[a * width + b]
                        for j in range(step):
                            term = k * xv[j]
                            acc[r][j] = term if acc[r][j] is None else acc[r][j] + term
        for r in range(rows):
            for j in range(step):
                out[r, pl.ds(j0 + j, SUB, stride=per), :] = acc[r][j]


def spread_taps(kb, kernel_ref, lanes, width):
    for a in range(width):
        row = kernel_ref[a, :, lanes]
        for b in range(width):
            kb[a * width + b] = jnp.broadcast_to(row[b : b + 1], (SUB, LANES))


def forward_conv_kernel(
    inner, mid, outer, kernel_ref, normed_bf, normed, inv_out, xs, kb, conv
):
    rows, cols, channels = mid.shape
    rad = inner.shape[0]
    blocks = channels // LANES
    zero_edges(xs, rows, rad, cols)

    def block(cb, _):
        lanes = pl.ds(pl.multiple_of(cb * LANES, LANES), LANES)
        fill_padded(xs, inner, mid, outer, rows, rad, cols, lanes)
        spread_taps(kb, kernel_ref, lanes, 2 * rad + 1)
        taps(xs, kb, conv.at[cb], rows, rad, cols, False)
        return 0

    lax.fori_loop(0, blocks, block, 0)

    def norm(r, _):
        total = conv[0, r]
        for cb in range(1, blocks):
            total = total + conv[cb, r]
        mean_u = jnp.sum(total, -1, keepdims=True) * (1.0 / channels)
        square = jnp.zeros((cols, LANES), F32)
        for cb in range(blocks):
            centred = conv[cb, r] - mean_u
            square = square + centred * centred
        var = jnp.sum(square, -1, keepdims=True) * (1.0 / channels)
        inv_std = lax.rsqrt(var + 1e-06)
        for cb in range(blocks):
            value = (conv[cb, r] - mean_u) * inv_std
            normed[r, :, cb * LANES : (cb + 1) * LANES] = value
            normed_bf[r, :, cb * LANES : (cb + 1) * LANES] = value.astype(BF16)
        inv_out[r] = inv_std
        return 0

    lax.fori_loop(0, rows, norm, 0)


def backward_conv_kernel(inner, mid, outer, kernel_ref, cot, out, xs, kb, conv):
    rows, cols, channels = mid.shape
    rad = inner.shape[0]
    zero_edges(xs, rows, rad, cols)

    def block(cb, _):
        lanes = pl.ds(pl.multiple_of(cb * LANES, LANES), LANES)
        fill_padded(xs, inner, mid, outer, rows, rad, cols, lanes)
        spread_taps(kb, kernel_ref, lanes, 2 * rad + 1)
        taps(xs, kb, conv, rows, rad, cols, True)
        out[:, :, lanes] = (cot[:, :, lanes].astype(F32) + conv[...]).astype(BF16)
        return 0

    lax.fori_loop(0, channels // LANES, block, 0)


def conv_scratch(rows, rad, cols):
    width = 2 * rad + 1
    return [
        pltpu.VMEM((rows + 2 * rad, cols + 2 * SUB, LANES), F32),
        pltpu.VMEM((width * width, SUB, LANES), F32),
    ]


def forward_conv(inner, mid, outer, kernel):
    rows, cols, channels = mid.shape
    rad = inner.shape[0]
    return pl.pallas_call(
        forward_conv_kernel,
        name="forward_conv",
        out_shape=(
            jax.ShapeDtypeStruct(mid.shape, BF16),
            jax.ShapeDtypeStruct(mid.shape, F32),
            jax.ShapeDtypeStruct((rows, cols, 1), F32),
        ),
        in_specs=[VMEM] * 4,
        out_specs=(VMEM,) * 3,
        scratch_shapes=conv_scratch(rows, rad, cols)
        + [pltpu.VMEM((channels // LANES, rows, cols, LANES), F32)],
        compiler_params=pltpu.CompilerParams(vmem_limit_bytes=KERNEL_VMEM),
        cost_estimate=pl.CostEstimate(
            flops=2 * mid.size * kernel.shape[0] * kernel.shape[1],
            bytes_accessed=8 * mid.size,
            transcendentals=0,
        ),
    )(inner, mid, outer, kernel)


def backward_conv(inner, mid, outer, kernel, cot):
    rows, cols, _ = mid.shape
    rad = inner.shape[0]
    return pl.pallas_call(
        backward_conv_kernel,
        name="backward_conv",
        out_shape=jax.ShapeDtypeStruct(mid.shape, BF16),
        in_specs=[VMEM] * 5,
        out_specs=VMEM,
        scratch_shapes=conv_scratch(rows, rad, cols) + [pltpu.VMEM((rows, cols, LANES), F32)],
        compiler_params=pltpu.CompilerParams(vmem_limit_bytes=KERNEL_VMEM),
        cost_estimate=pl.CostEstimate(
            flops=2 * mid.size * kernel.shape[0] * kernel.shape[1],
            bytes_accessed=6 * mid.size,
            transcendentals=0,
        ),
    )(inner, mid, outer, kernel, cot)


def lay_out(win, wout, pieces, offs, size, r):
    ratio, m = win.shape[1] // wout.shape[1], wout.shape[1] // size
    shard = win.shape[3]
    me, parity = member(size)
    for piece, off in zip(pieces, offs):
        pos = place(me, parity, off)
        for q in range(ratio):
            columns = slice(q * shard, (q + 1) * shard)
            win[r, pl.ds((pos * ratio + q) * m, m)] = piece[r, 0, :, :, columns]
        wout[r, pl.ds(pos * m, m)] = piece[r, 1]


def hidden_kernel(layout, slots, g, n, *refs):
    normed_ref, cot_ref = refs[:2]
    weights = refs[2 : 2 + n]
    activ, d_pre, keep, send = refs[2 + n : 6 + n]
    grad = refs[-1]
    _, channels = normed_ref.shape
    shard = activ.shape[2]
    me, parity = member(g)
    normed = normed_ref[...]
    normed_t = normed.T
    cot = cot_ref[...]
    for r in range(activ.shape[0]):
        if layout is None:
            w_in, w_out = weights[0][...], weights[1][...]
        else:
            win, wout = refs[6 + n : 8 + n]
            lay_out(win, wout, weights, layout[0], layout[1], r)
            w_in = win[r].reshape(channels, shard)
            w_out = wout[r].reshape(shard, channels)
        pre = contract(normed, w_in, 1, 0)
        d_hidden = contract(cot, w_out, 1, 1)
        cdf = normal_cdf(pre)
        activ[r] = (pre * cdf).astype(BF16)
        slope = cdf + pre * jnp.exp(-0.5 * pre * pre) * 0.3989422804014327
        d_p = (d_hidden * slope).astype(BF16)
        d_pre[r] = d_p
        grad[...] = contract(normed_t, d_p, 1, 0).astype(BF16).reshape(grad.shape)
        for target, offsets in zip((keep, send), slots):
            for idx, off in enumerate(offsets):
                target[idx, r] = grad[place(me, parity, off)]


def input_grad_kernel(counts, *refs):
    parts = len(counts)
    acts, d_pres = refs[:parts], refs[parts : 2 * parts]
    terrain, normed, inv_std = refs[2 * parts : 2 * parts + 3]
    weights = refs[2 * parts + 3 : -2]
    output, d_conv = refs[-2:]
    channels = normed.shape[1]
    shard = acts[0].shape[2]
    mixed = d_normed = None
    for i, count in enumerate(counts):
        for r in range(count):
            if i == 0:
                w_in, w_out = weights[0][...], weights[1][...]
            else:
                w_in = weights[2 * i][r].reshape(channels, shard)
                w_out = weights[2 * i + 1][r].reshape(shard, channels)
            dn = contract(d_pres[i][r], w_in, 1, 1)
            mx = contract(acts[i][r], w_out, 1, 0)
            mixed = mx if mixed is None else mixed + mx
            d_normed = dn if d_normed is None else d_normed + dn
    output[...] = (terrain[...].astype(F32) + mixed).astype(BF16)
    unit = normed[...]
    mean_d = jnp.sum(d_normed, -1, keepdims=True) * (1.0 / channels)
    mean_dn = jnp.sum(d_normed * unit, -1, keepdims=True) * (1.0 / channels)
    d_conv[...] = (inv_std[...] * (d_normed - mean_d - unit * mean_dn)).astype(BF16)


def hidden_stage(ex, normed, cot, weights, layout, count):
    pixels, channels = normed.shape
    g = ex.g
    shard = weights[0].shape[1]
    if layout is not None:
        shard = layout[1] * weights[0].shape[2] * weights[0].shape[3]
    rows = shard // g
    slots = (ex.keep_offsets(), ex.send_offsets()) if g > 1 else (ex.keep_offsets(),)
    part = jax.ShapeDtypeStruct((ex.chips(), count, channels // g, shard), BF16)
    per_unit = jax.ShapeDtypeStruct((count, pixels, shard), BF16)
    outs = [per_unit, per_unit, part, part]
    if layout is not None:
        outs.append(jax.ShapeDtypeStruct((count, channels // rows, rows, shard), BF16))
        outs.append(jax.ShapeDtypeStruct((count, g, rows, channels), BF16))
    return pl.pallas_call(
        functools.partial(hidden_kernel, layout, slots, g, len(weights)),
        name="hidden_stage",
        out_shape=tuple(outs),
        in_specs=[VMEM] * (2 + len(weights)),
        out_specs=(VMEM,) * len(outs),
        scratch_shapes=[pltpu.VMEM((g, channels // g, shard), BF16)],
        compiler_params=pltpu.CompilerParams(vmem_limit_bytes=KERNEL_VMEM),
        cost_estimate=pl.CostEstimate(
            flops=6 * pixels * channels * shard * count,
            bytes_accessed=8 * channels * shard * count,
            transcendentals=2 * pixels * shard * count,
        ),
    )(normed, cot, *weights)


def input_grad_stage(acts, d_pres, terrain, normed, inv_std, weights):
    pixels, channels = normed.shape
    counts = tuple(a.shape[0] for a in acts)
    units = sum(counts) * acts[0].shape[2]
    flat = jax.ShapeDtypeStruct((pixels, channels), BF16)
    return pl.pallas_call(
        functools.partial(input_grad_kernel, counts),
        name="input_grad_stage",
        out_shape=(flat, flat),
        in_specs=[VMEM] * (2 * len(acts) + 3 + len(weights)),
        out_specs=(VMEM, VMEM),
        compiler_params=pltpu.CompilerParams(vmem_limit_bytes=KERNEL_VMEM),
        cost_estimate=pl.CostEstimate(
            flops=4 * pixels * channels * units,
            bytes_accessed=4 * channels * units,
            transcendentals=0,
        ),
    )(*acts, *d_pres, terrain, normed, inv_std, *weights)


def final_kernel(offs, g, scale, *refs):
    out = refs[-1]
    me, parity = member(g)
    for block, off in zip(refs[:-1], offs):
        out[place(me, parity, off)] = block[...].astype(F32) * scale


def final_stage(ex, blocks, offs, scale):
    rows, shard = blocks[0].shape
    return pl.pallas_call(
        functools.partial(final_kernel, offs, ex.g, scale),
        name="final_stage",
        out_shape=jax.ShapeDtypeStruct((ex.g, rows, shard), F32),
        in_specs=[VMEM] * len(blocks),
        out_specs=VMEM,
        compiler_params=pltpu.CompilerParams(vmem_limit_bytes=KERNEL_VMEM),
        cost_estimate=pl.CostEstimate(
            flops=ex.g * rows * shard, bytes_accessed=6 * ex.g * rows * shard, transcendentals=0
        ),
    )(*blocks)


def add(first, *rest):
    total = first.astype(F32)
    for term in rest:
        total = total + term.astype(F32)
    return total.astype(BF16)


def halo(x, rad):
    peers = lax.axis_size("tile")
    odd = lax.rem(lax.axis_index("tile"), 2)
    span = x.shape[0] - rad
    to_inner = lax.dynamic_slice_in_dim(x, (1 - odd) * span, rad)
    to_outer = lax.dynamic_slice_in_dim(x, odd * span, rad)

    def swaps(start):
        pairs = [(i, i + 1) for i in range(start, peers - 1, 2)]
        return pairs + [(j, i) for i, j in pairs]

    outer = lax.ppermute(to_outer, "tile", swaps(1))
    inner = lax.ppermute(to_inner, "tile", swaps(0))
    return inner, outer


def block(terrain, kernel, w_in, w_out, cotangent):
    scenes, height, breadth, channels = terrain.shape
    pixels = scenes * height * breadth
    shard = w_in.shape[1]
    rad = kernel.shape[0] // 2
    tiles, scens = lax.axis_size("tile"), lax.axis_size("scen")
    g = group_size(tiles, channels, shard)
    ex = Exchange(tiles, scens, g)
    rows = shard // g
    ratio = channels // shard

    def piece(size):
        me = lax.rem(lax.axis_index("tile"), size)
        first = w_in.reshape(size, ratio, shard // size, shard)[me]
        first = jnp.concatenate([first[q] for q in range(ratio)], axis=-1)
        both = jnp.stack([first, w_out.reshape(size, shard // size, channels)[me]])
        return both.reshape(2, g // size, rows, channels)

    near, far = list(range(1, min(2, scens))), list(range(2, scens))
    stages = [("own", (w_in, w_out), None, 1)]
    far_stage = []
    if far:
        own = piece(g)
        got = jnp.stack([ex.fetch(own, r) for r in far])
        items, offs = ex.gather(got, False)
        far_stage.append(("far", items, (tuple(offs), g), len(far)))
    if near:
        size = min(g, 2)
        got = ex.fetch(piece(size), near[0])[None]
        items, offs = [got], [(0, 0)]
        if size > 1:
            items.append(ex.core(got))
            offs.append((1, 1))
        stages.append(("near", items, (tuple(offs), size), 1))
    stages += far_stage

    image = terrain.reshape(height, breadth, channels)
    inner, outer = halo(image, rad)
    normed_bf, normed, inv_std = forward_conv(inner, image, outer, kernel)
    normed_bf = normed_bf.reshape(pixels, channels)
    normed = normed.reshape(pixels, channels)
    inv_std = inv_std.reshape(pixels, 1)
    cot = cotangent.reshape(pixels, channels)

    acts, d_pres, weights, parts = [], [], [], []
    to_own = []
    for name, arrays, layout, count in stages:
        activ, d_pre, keep, send, *laid = hidden_stage(ex, normed_bf, cot, arrays, layout, count)
        acts.append(activ)
        d_pres.append(d_pre)
        weights += laid if laid else arrays
        pair = [keep, ex.core(send)] if g > 1 else [keep]
        if name == "own":
            to_own += [p[:, 0] for p in pair]
        elif name == "near":
            to_own.append(ex.deliver(add(*[p[:, 0] for p in pair]), near[0]))
        else:
            parts.append([add(*[p[i] for p in pair]) for i in range(ex.chips())])
    parts.insert(0, [add(*[p[i] for p in to_own])[None] for i in range(ex.chips())])
    parts = [jnp.concatenate(p) for p in zip(*parts)]
    summed = parts[0].astype(F32)
    for i in range(1, ex.chips()):
        summed = summed + ex.hop(parts[i], i).astype(F32)
    total = summed[0]
    for i, r in enumerate(far):
        total = total + ex.deliver(summed[1 + i].astype(BF16), r).astype(F32)
    if tiles > g:
        members = [[i + g * k for k in range(tiles // g)] for i in range(g)]
        total = lax.psum(total, "tile", axis_index_groups=members)
    blocks, block_offs = ex.gather(total.astype(BF16), True)

    output, d_conv = input_grad_stage(
        acts, d_pres, terrain.reshape(pixels, channels), normed, inv_std, weights
    )
    d_image = d_conv.reshape(height, breadth, channels)
    d_inner, d_outer = halo(d_image, rad)
    d_terrain = backward_conv(
        d_inner, d_image, d_outer, kernel, cotangent.reshape(height, breadth, channels)
    )

    scale = 1.0 / math.sqrt(pixels * tiles * scens)
    grad_in = final_stage(ex, blocks, block_offs, scale)
    return (
        output.reshape(terrain.shape),
        d_terrain.reshape(terrain.shape),
        grad_in.reshape(channels, shard),
    )


def solution(mesh):
    return jax.shard_map(
        block,
        mesh=mesh,
        in_specs=(
            P("scen", "tile", None, None),
            P(),
            P(None, "scen"),
            P("scen", None),
            P("scen", "tile", None, None),
        ),
        out_specs=(P("scen", "tile", None, None), P("scen", "tile", None, None), P(None, "scen")),
        check_vma=False,
    )
```

```python
import functools
import math

import jax
import jax.numpy as jnp
from jax import lax
from jax.experimental import pallas as pl
from jax.experimental.pallas import tpu as pltpu
from jax.sharding import PartitionSpec as P


KERNEL_VMEM = 24 << 20
LANES = 128
SUB = 8
PACK = 16
VMEM = pl.BlockSpec(memory_space=pltpu.VMEM)
ANY = pl.BlockSpec(memory_space=pl.ANY)
F32 = jnp.float32
BF16 = jnp.bfloat16


def group_size(tiles, channels, shard):
    g = 1
    while tiles % (2 * g) == 0 and channels % (2 * g * PACK) == 0 and shard % (2 * g * PACK) == 0:
        g *= 2
    return g


class Exchange:
    def __init__(self, tiles, scens, g):
        self.tiles, self.scens, self.g = tiles, scens, g
        self.bits = [1 << i for i in range(1, g.bit_length() - 1)]
        self.stages = len(self.bits)

    def offset(self, idx, parity):
        off = 0
        for j in range(self.stages):
            if idx >> j & 1:
                off ^= self.bits[j] if parity == 0 else self.bits[self.stages - 1 - j]
        return off

    def chips(self):
        return 1 << self.stages

    def hop(self, x, idx):
        perm = [(t, t ^ self.offset(idx, t % 2)) for t in range(self.tiles)]
        return lax.ppermute(x, "tile", perm)

    def core(self, x):
        return lax.ppermute(x, "tile", [(t, t ^ 1) for t in range(self.tiles)])

    def plane(self, z, r):
        if self.scens & (self.scens - 1) == 0:
            return z ^ r
        return (z + r) % self.scens

    def fetch(self, x, r):
        return lax.ppermute(x, "scen", [(self.plane(z, r), z) for z in range(self.scens)])

    def deliver(self, x, r):
        return lax.ppermute(x, "scen", [(z, self.plane(z, r)) for z in range(self.scens)])

    def keep_offsets(self):
        return [(self.offset(i, 0), self.offset(i, 1)) for i in range(self.chips())]

    def send_offsets(self):
        return [(1 ^ o[1], 1 ^ o[0]) for o in self.keep_offsets()]

    def gather(self, x, direct):
        items = [x]
        if direct:
            items += [self.hop(x, i) for i in range(1, self.chips())]
        else:
            for j in range(self.stages):
                items += [self.hop(a, 1 << j) for a in items]
        offs = self.keep_offsets()
        if self.g > 1:
            items += [self.core(a) for a in items]
            offs = offs + self.send_offsets()
        return items, offs


def member(g):
    t = lax.axis_index("tile")
    return lax.rem(t, g), lax.rem(t, 2)


def place(me, parity, off):
    return me ^ jnp.where(parity == 0, off[0], off[1])


def normal_cdf(values):
    return 0.5 * (1.0 + lax.erf(values * 0.7071067811865476))


def contract(a, b, da, db):
    return lax.dot_general(a, b, (((da,), (db,)), ((), ())), preferred_element_type=F32)


def fill_padded(xs, inner, mid, outer, rows, rad, cols, lanes):
    odd = lax.rem(lax.axis_index("tile"), 2)
    columns = slice(SUB, SUB + cols)
    xs[pl.ds((1 - odd) * (rad + rows), rad), columns, :] = inner[:, :, lanes].astype(F32)
    xs[pl.ds(odd * (rad + rows), rad), columns, :] = outer[:, :, lanes].astype(F32)
    xs[rad : rad + rows, columns, :] = mid[:, :, lanes].astype(F32)


def zero_edges(xs, rows, rad, cols):
    edge = jnp.zeros((rows + 2 * rad, SUB, LANES), F32)
    xs[:, 0:SUB, :] = edge
    xs[:, SUB + cols : 2 * SUB + cols, :] = edge


def taps(xs, kb, out, rows, rad, cols, flip):
    width = 2 * rad + 1
    per = cols // SUB
    step = 4 if per % 4 == 0 else 1
    for j0 in range(0, per, step):
        acc = [[None] * step for _ in range(rows)]
        for b in range(width):
            for src in range(rows + 2 * rad):
                xv = [
                    xs[src, pl.ds(SUB + j0 + j + b - rad, SUB, stride=per), :] for j in range(step)
                ]
                for r in range(rows):
                    a = src - r
                    if 0 <= a < width:
                        k = kb[width * width - 1 - (a * width + b)] if flip else kb[a * width + b]
                        for j in range(step):
                            term = k * xv[j]
                            acc[r][j] = term if acc[r][j] is None else acc[r][j] + term
        for r in range(rows):
            for j in range(step):
                out[r, pl.ds(j0 + j, SUB, stride=per), :] = acc[r][j]


def spread_taps(kb, kernel_ref, lanes, width):
    for a in range(width):
        row = kernel_ref[a, :, lanes]
        for b in range(width):
            kb[a * width + b] = jnp.broadcast_to(row[b : b + 1], (SUB, LANES))


def forward_conv_kernel(
    inner, mid, outer, kernel_ref, normed_bf, normed, inv_out, xs, kb, conv
):
    rows, cols, channels = mid.shape
    rad = inner.shape[0]
    blocks = channels // LANES
    zero_edges(xs, rows, rad, cols)

    def block(cb, _):
        lanes = pl.ds(pl.multiple_of(cb * LANES, LANES), LANES)
        fill_padded(xs, inner, mid, outer, rows, rad, cols, lanes)
        spread_taps(kb, kernel_ref, lanes, 2 * rad + 1)
        taps(xs, kb, conv.at[cb], rows, rad, cols, False)
        return 0

    lax.fori_loop(0, blocks, block, 0)

    def norm(r, _):
        total = conv[0, r]
        for cb in range(1, blocks):
            total = total + conv[cb, r]
        mean_u = jnp.sum(total, -1, keepdims=True) * (1.0 / channels)
        square = jnp.zeros((cols, LANES), F32)
        for cb in range(blocks):
            centred = conv[cb, r] - mean_u
            square = square + centred * centred
        var = jnp.sum(square, -1, keepdims=True) * (1.0 / channels)
        inv_std = lax.rsqrt(var + 1e-06)
        for cb in range(blocks):
            value = (conv[cb, r] - mean_u) * inv_std
            normed[r, :, cb * LANES : (cb + 1) * LANES] = value
            normed_bf[r, :, cb * LANES : (cb + 1) * LANES] = value.astype(BF16)
        inv_out[r] = inv_std
        return 0

    lax.fori_loop(0, rows, norm, 0)


def backward_conv_kernel(inner, mid, outer, kernel_ref, cot, out, xs, kb, conv):
    rows, cols, channels = mid.shape
    rad = inner.shape[0]
    zero_edges(xs, rows, rad, cols)

    def block(cb, _):
        lanes = pl.ds(pl.multiple_of(cb * LANES, LANES), LANES)
        fill_padded(xs, inner, mid, outer, rows, rad, cols, lanes)
        spread_taps(kb, kernel_ref, lanes, 2 * rad + 1)
        taps(xs, kb, conv, rows, rad, cols, True)
        out[:, :, lanes] = (cot[:, :, lanes].astype(F32) + conv[...]).astype(BF16)
        return 0

    lax.fori_loop(0, channels // LANES, block, 0)


def conv_scratch(rows, rad, cols):
    width = 2 * rad + 1
    return [
        pltpu.VMEM((rows + 2 * rad, cols + 2 * SUB, LANES), F32),
        pltpu.VMEM((width * width, SUB, LANES), F32),
    ]


def forward_conv(inner, mid, outer, kernel):
    rows, cols, channels = mid.shape
    rad = inner.shape[0]
    return pl.pallas_call(
        forward_conv_kernel,
        name="forward_conv",
        out_shape=(
            jax.ShapeDtypeStruct(mid.shape, BF16),
            jax.ShapeDtypeStruct(mid.shape, F32),
            jax.ShapeDtypeStruct((rows, cols, 1), F32),
        ),
        in_specs=[VMEM] * 4,
        out_specs=(VMEM,) * 3,
        scratch_shapes=conv_scratch(rows, rad, cols)
        + [pltpu.VMEM((channels // LANES, rows, cols, LANES), F32)],
        compiler_params=pltpu.CompilerParams(vmem_limit_bytes=KERNEL_VMEM),
        cost_estimate=pl.CostEstimate(
            flops=2 * mid.size * kernel.shape[0] * kernel.shape[1],
            bytes_accessed=8 * mid.size,
            transcendentals=0,
        ),
    )(inner, mid, outer, kernel)


def backward_conv(inner, mid, outer, kernel, cot):
    rows, cols, _ = mid.shape
    rad = inner.shape[0]
    return pl.pallas_call(
        backward_conv_kernel,
        name="backward_conv",
        out_shape=jax.ShapeDtypeStruct(mid.shape, BF16),
        in_specs=[VMEM] * 5,
        out_specs=VMEM,
        scratch_shapes=conv_scratch(rows, rad, cols) + [pltpu.VMEM((rows, cols, LANES), F32)],
        compiler_params=pltpu.CompilerParams(vmem_limit_bytes=KERNEL_VMEM),
        cost_estimate=pl.CostEstimate(
            flops=2 * mid.size * kernel.shape[0] * kernel.shape[1],
            bytes_accessed=6 * mid.size,
            transcendentals=0,
        ),
    )(inner, mid, outer, kernel, cot)


def lay_out(win, wout, pieces, offs, size, r):
    ratio, m = win.shape[1] // wout.shape[1], wout.shape[1] // size
    shard = win.shape[3]
    me, parity = member(size)
    for piece, off in zip(pieces, offs):
        pos = place(me, parity, off)
        for q in range(ratio):
            columns = slice(q * shard, (q + 1) * shard)
            win[r, pl.ds((pos * ratio + q) * m, m)] = piece[r, 0, :, :, columns]
        wout[r, pl.ds(pos * m, m)] = piece[r, 1]


def hidden_kernel(layout, slots, g, n, *refs):
    normed_ref, cot_ref = refs[:2]
    weights = refs[2 : 2 + n]
    activ, d_pre, keep, send = refs[2 + n : 6 + n]
    grad = refs[-1]
    _, channels = normed_ref.shape
    shard = activ.shape[2]
    me, parity = member(g)
    normed = normed_ref[...]
    normed_t = normed.T
    cot = cot_ref[...]
    for r in range(activ.shape[0]):
        if layout is None:
            w_in, w_out = weights[0][...], weights[1][...]
        else:
            win, wout = refs[6 + n : 8 + n]
            lay_out(win, wout, weights, layout[0], layout[1], r)
            w_in = win[r].reshape(channels, shard)
            w_out = wout[r].reshape(shard, channels)
        pre = contract(normed, w_in, 1, 0)
        d_hidden = contract(cot, w_out, 1, 1)
        cdf = normal_cdf(pre)
        activ[r] = (pre * cdf).astype(BF16)
        slope = cdf + pre * jnp.exp(-0.5 * pre * pre) * 0.3989422804014327
        d_p = (d_hidden * slope).astype(BF16)
        d_pre[r] = d_p
        grad[...] = contract(normed_t, d_p, 1, 0).astype(BF16).reshape(grad.shape)
        for target, offsets in zip((keep, send), slots):
            for idx, off in enumerate(offsets):
                target[idx, r] = grad[place(me, parity, off)]


def input_grad_kernel(counts, *refs):
    parts = len(counts)
    acts, d_pres = refs[:parts], refs[parts : 2 * parts]
    terrain, normed, inv_std = refs[2 * parts : 2 * parts + 3]
    weights = refs[2 * parts + 3 : -2]
    output, d_conv = refs[-2:]
    channels = normed.shape[1]
    shard = acts[0].shape[2]
    mixed = d_normed = None
    for i, count in enumerate(counts):
        for r in range(count):
            w_in, w_out = weights[2 * i], weights[2 * i + 1]
            if len(w_in.shape) == 2:
                w_in, w_out = w_in[...], w_out[...]
            else:
                w_in = w_in[r].reshape(channels, shard)
                w_out = w_out[r].reshape(shard, channels)
            dn = contract(d_pres[i][r], w_in, 1, 1)
            mx = contract(acts[i][r], w_out, 1, 0)
            mixed = mx if mixed is None else mixed + mx
            d_normed = dn if d_normed is None else d_normed + dn
    output[...] = (terrain[...].astype(F32) + mixed).astype(BF16)
    unit = normed[...]
    mean_d = jnp.sum(d_normed, -1, keepdims=True) * (1.0 / channels)
    mean_dn = jnp.sum(d_normed * unit, -1, keepdims=True) * (1.0 / channels)
    d_conv[...] = (inv_std[...] * (d_normed - mean_d - unit * mean_dn)).astype(BF16)


def hidden_stage(ex, normed, cot, weights, layout, count):
    pixels, channels = normed.shape
    g = ex.g
    shard = weights[0].shape[1]
    if layout is not None:
        shard = layout[1] * weights[0].shape[2] * weights[0].shape[3]
    rows = shard // g
    slots = (ex.keep_offsets(), ex.send_offsets()) if g > 1 else (ex.keep_offsets(),)
    part = jax.ShapeDtypeStruct((ex.chips(), count, channels // g, shard), BF16)
    per_unit = jax.ShapeDtypeStruct((count, pixels, shard), BF16)
    outs = [per_unit, per_unit, part, part]
    if layout is not None:
        outs.append(jax.ShapeDtypeStruct((count, channels // rows, rows, shard), BF16))
        outs.append(jax.ShapeDtypeStruct((count, g, rows, channels), BF16))
    return pl.pallas_call(
        functools.partial(hidden_kernel, layout, slots, g, len(weights)),
        name="hidden_stage",
        out_shape=tuple(outs),
        in_specs=[VMEM] * (2 + len(weights)),
        out_specs=(VMEM,) * len(outs),
        scratch_shapes=[pltpu.VMEM((g, channels // g, shard), BF16)],
        compiler_params=pltpu.CompilerParams(vmem_limit_bytes=KERNEL_VMEM),
        cost_estimate=pl.CostEstimate(
            flops=6 * pixels * channels * shard * count,
            bytes_accessed=8 * channels * shard * count,
            transcendentals=2 * pixels * shard * count,
        ),
    )(normed, cot, *weights)


def input_grad_stage(acts, d_pres, terrain, normed, inv_std, weights):
    pixels, channels = normed.shape
    counts = tuple(a.shape[0] for a in acts)
    weights = [w for pair in weights for w in pair]
    units = sum(counts) * acts[0].shape[2]
    flat = jax.ShapeDtypeStruct((pixels, channels), BF16)
    return pl.pallas_call(
        functools.partial(input_grad_kernel, counts),
        name="input_grad_stage",
        out_shape=(flat, flat),
        in_specs=[VMEM] * (2 * len(acts) + 3 + len(weights)),
        out_specs=(VMEM, VMEM),
        compiler_params=pltpu.CompilerParams(vmem_limit_bytes=KERNEL_VMEM),
        cost_estimate=pl.CostEstimate(
            flops=4 * pixels * channels * units,
            bytes_accessed=4 * channels * units,
            transcendentals=0,
        ),
    )(*acts, *d_pres, terrain, normed, inv_std, *weights)


def final_kernel(offs, g, scale, *refs):
    out = refs[-1]
    me, parity = member(g)
    for block, off in zip(refs[:-1], offs):
        out[place(me, parity, off)] = block[...].astype(F32) * scale


def final_stage(ex, blocks, offs, scale):
    rows, shard = blocks[0].shape
    return pl.pallas_call(
        functools.partial(final_kernel, offs, ex.g, scale),
        name="final_stage",
        out_shape=jax.ShapeDtypeStruct((ex.g, rows, shard), F32),
        in_specs=[VMEM] * len(blocks),
        out_specs=VMEM,
        compiler_params=pltpu.CompilerParams(vmem_limit_bytes=KERNEL_VMEM),
        cost_estimate=pl.CostEstimate(
            flops=ex.g * rows * shard, bytes_accessed=6 * ex.g * rows * shard, transcendentals=0
        ),
    )(*blocks)


def add(first, *rest):
    total = first.astype(F32)
    for term in rest:
        total = total + term.astype(F32)
    return total.astype(BF16)


def halo(x, rad):
    peers = lax.axis_size("tile")
    odd = lax.rem(lax.axis_index("tile"), 2)
    span = x.shape[0] - rad
    to_inner = lax.dynamic_slice_in_dim(x, (1 - odd) * span, rad)
    to_outer = lax.dynamic_slice_in_dim(x, odd * span, rad)

    def swaps(start):
        pairs = [(i, i + 1) for i in range(start, peers - 1, 2)]
        return pairs + [(j, i) for i, j in pairs]

    outer = lax.ppermute(to_outer, "tile", swaps(1))
    inner = lax.ppermute(to_inner, "tile", swaps(0))
    return inner, outer


def block(terrain, kernel, w_in, w_out, cotangent):
    scenes, height, breadth, channels = terrain.shape
    pixels = scenes * height * breadth
    shard = w_in.shape[1]
    rad = kernel.shape[0] // 2
    tiles, scens = lax.axis_size("tile"), lax.axis_size("scen")
    g = group_size(tiles, channels, shard)
    ex = Exchange(tiles, scens, g)
    rows = shard // g
    ratio = channels // shard

    def piece(size):
        me = lax.rem(lax.axis_index("tile"), size)
        first = w_in.reshape(size, ratio, shard // size, shard)[me]
        first = jnp.concatenate([first[q] for q in range(ratio)], axis=-1)
        both = jnp.stack([first, w_out.reshape(size, shard // size, channels)[me]])
        return both.reshape(2, g // size, rows, channels)

    stages = {0: ((w_in, w_out), None, [0])}
    if scens > 2:
        own = piece(g)
        for i, ranks in enumerate(far_groups(scens), 2):
            got = jnp.stack([ex.fetch(own, r) for r in ranks])
            items, offs = ex.gather(got, True)
            stages[i] = (items, (tuple(offs), g), ranks)
    if scens > 1:
        size = min(g, 2)
        got = ex.fetch(piece(size), 1)[None]
        items, offs = [got], [(0, 0)]
        if size > 1:
            items.append(ex.core(got))
            offs.append((1, 1))
        stages[1] = (items, (tuple(offs), size), [1])

    image = terrain.reshape(height, breadth, channels)
    inner, outer = halo(image, rad)
    normed_bf, normed, inv_std = forward_conv(inner, image, outer, kernel)
    normed_bf = normed_bf.reshape(pixels, channels)
    normed = normed.reshape(pixels, channels)
    inv_std = inv_std.reshape(pixels, 1)
    cot = cotangent.reshape(pixels, channels)

    acts, d_pres, weights, to_own, parts = [], [], [], [], []
    for i in sorted(stages):
        arrays, layout, ranks = stages[i]
        activ, d_pre, keep, send, *laid = hidden_stage(
            ex, normed_bf, cot, arrays, layout, len(ranks)
        )
        acts.append(activ)
        d_pres.append(d_pre)
        weights.append(laid if laid else arrays)
        pair = [keep, ex.core(send)] if g > 1 else [keep]
        if i == 0:
            to_own += [p[:, 0] for p in pair]
        elif i == 1:
            to_own.append(ex.deliver(add(*[p[:, 0] for p in pair]), 1))
        else:
            parts.append([add(*[p[c] for p in pair]) for c in range(ex.chips())])
    parts.insert(0, [add(*[p[c] for p in to_own])[None] for c in range(ex.chips())])
    parts = [jnp.concatenate(p) for p in zip(*parts)]
    summed = parts[0].astype(F32)
    for c in range(1, ex.chips()):
        summed = summed + ex.hop(parts[c], c).astype(F32)
    total = summed[0]
    for c, r in enumerate(range(2, scens), 1):
        total = total + ex.deliver(summed[c].astype(BF16), r).astype(F32)
    if tiles > g:
        members = [[i + g * k for k in range(tiles // g)] for i in range(g)]
        total = lax.psum(total, "tile", axis_index_groups=members)
    blocks, block_offs = ex.gather(total.astype(BF16), True)

    output, d_conv = input_grad_stage(
        acts,
        d_pres,
        terrain.reshape(pixels, channels),
        normed,
        inv_std,
        weights,
    )
    d_image = d_conv.reshape(height, breadth, channels)
    d_inner, d_outer = halo(d_image, rad)
    d_terrain = backward_conv(
        d_inner, d_image, d_outer, kernel, cotangent.reshape(height, breadth, channels)
    )

    scale = 1.0 / math.sqrt(pixels * tiles * scens)
    grad_in = final_stage(ex, blocks, block_offs, scale)
    return (
        output.reshape(terrain.shape),
        d_terrain.reshape(terrain.shape),
        grad_in.reshape(channels, shard),
    )


def far_groups(scens):
    return [list(range(2, scens))]


def solution(mesh):
    return jax.shard_map(
        block,
        mesh=mesh,
        in_specs=(
            P("scen", "tile", None, None),
            P(),
            P(None, "scen"),
            P("scen", None),
            P("scen", "tile", None, None),
        ),
        out_specs=(P("scen", "tile", None, None), P("scen", "tile", None, None), P(None, "scen")),
        check_vma=False,
    )
```
